256 devices in a mesh: tm: 4 (over x_hi, core), space: 64 (over x_lo, y, z).
Axes of the slice: x: 4 (x_hi: 2, x_lo: 2; x = x_hi * 2 + x_lo), y: 4, z: 8, core: 2. Of those that a mesh axis runs over, the one named last changes fastest.
Arguments:
- latent_tokens: bfloat16 [16, 64, 64, 64], P('tm', None, 'space'), may hold values from -12 to 12
- conv_in_weight: bfloat16 [3, 3, 3, 16, 384], replicated, may hold values from -0.3125 to 0.3125
- conv_in_bias: float32 [384], replicated, may hold values from -3 to 3
- norm_gain: float32 [384], replicated, may hold values from 0.25 to 1.75
- conv_mid_weight: bfloat16 [3, 3, 3, 384, 384], replicated, may hold values from -0.0625 to 0.0625
- conv_mid_bias: float32 [384], replicated, may hold values from -3 to 3
Outputs:
- decoded: bfloat16 [16, 128, 128, 384], P('tm', 'space')
The draws below stay inside these ranges and needn't reach their ends.
All inputs are finite; a program needn't handle non-finite values.
Results may differ from the reference program's by a relative error of at most 0.005.
Values may be sent and summed in bfloat16 or wider, within the bound.
A program may use at most 128 MiB of HBM per device.

```python
import math
import jax
import jax.numpy as jnp
from jax import lax

ZCH = 16
CMID = 384
TW = 64
FRAMES = 16
TH = 64


def draw_latent_tokens(key, part):
    shape = (FRAMES, TH, TW, 4, ZCH)
    scales = jnp.exp(jax.random.uniform(jax.random.fold_in(key, 301), (FRAMES, TH, TW, 4, 1), jnp.float32, math.log(0.3), math.log(3.0)))
    base = jnp.clip(jax.random.normal(jax.random.fold_in(key, 303), shape, jnp.float32), -4.0, 4.0)
    return (base * scales).reshape(FRAMES, TH, TW, 4 * ZCH).astype(jnp.bfloat16)


def scatter_about(own_key, shape, scale, limit, kind=jnp.bfloat16):
    array = jax.random.normal(own_key, shape, jnp.float32) * scale
    return jnp.minimum(jnp.maximum(array, -limit), limit).astype(kind)


def setup_inputs(seed: int = 0) -> dict:
    splits = jax.random.split(jax.random.key(seed), 7)
    latent_tokens = draw_latent_tokens(jax.random.fold_in(splits[6], 71), 0)
    conv_in_weight = scatter_about(splits[1], (3, 3, 3, ZCH, CMID), (27 * ZCH) ** -0.5, 0.3125)
    conv_in_bias = scatter_about(splits[2], (CMID,), 0.5, 3.0, jnp.float32)
    norm_gain = jnp.clip(1.0 + 0.15 * jax.random.normal(splits[3], (CMID,), jnp.float32), 0.25, 1.75)
    conv_mid_weight = scatter_about(splits[4], (3, 3, 3, CMID, CMID), (27 * CMID) ** -0.5, 0.0625)
    conv_mid_bias = scatter_about(splits[5], (CMID,), 0.5, 3.0, jnp.float32)
    return {"latent_tokens": latent_tokens, "conv_in_weight": conv_in_weight, "conv_in_bias": conv_in_bias, "norm_gain": norm_gain, "conv_mid_weight": conv_mid_weight, "conv_mid_bias": conv_mid_bias}


def causal_conv(padded, weight):
    frames = padded.shape[0] - 2
    height = padded.shape[1] - 2
    breadth = padded.shape[2] - 2
    summed = jnp.zeros((frames * height * breadth, weight.shape[-1]), jnp.float32)
    for tap_time in range(3):
        for tap_row in range(3):
            for tap_col in range(3):
                window = padded[tap_time:tap_time + frames, tap_row:tap_row + height, tap_col:tap_col + breadth]
                summed = summed + jnp.dot(window.reshape(-1, window.shape[-1]), weight[tap_time, tap_row, tap_col], preferred_element_type=jnp.float32)
    return summed.reshape(frames, height, breadth, weight.shape[-1])

def unpatch(tokens):
    frames, height, breadth, _ = tokens.shape
    grid = tokens.reshape(frames, height, breadth, 2, 2, -1).transpose(0, 1, 3, 2, 4, 5)
    return grid.reshape(frames, 2 * height, 2 * breadth, -1)

def activate(feature, norm_gain):
    values = feature.astype(jnp.float32)
    spread = jnp.sqrt(lax.optimization_barrier(jnp.mean(values * values, axis=-1, keepdims=True)) + 1e-06)
    return jax.nn.silu(values / spread * norm_gain).astype(jnp.bfloat16)

def framewise(source, weight):
    padded = jnp.pad(source, ((2, 0), (1, 1), (1, 1), (0, 0)))

    def one_frame(start):
        window = lax.dynamic_slice_in_dim(padded, start, 3, 0)
        return causal_conv(window, weight)[0]
    return lax.map(one_frame, jnp.arange(source.shape[0], dtype=jnp.int32))

def reference(latent_tokens, conv_in_weight, conv_in_bias, norm_gain, conv_mid_weight, conv_mid_bias):
    latents = unpatch(latent_tokens)
    feature = (framewise(latents, conv_in_weight) + conv_in_bias).astype(jnp.bfloat16)
    activated = activate(feature, norm_gain)
    mixed_sum = framewise(activated, conv_mid_weight)
    decoded = (feature.astype(jnp.float32) + mixed_sum + conv_mid_bias).astype(jnp.bfloat16)
    return decoded
```

```python
import functools

import jax
import jax.numpy as jnp
from jax import lax
from jax.experimental import pallas as pl
from jax.experimental.pallas import tpu as pltpu
from jax.sharding import PartitionSpec as P

MESH = pl.DeviceIdType.MESH
C = 384
LAT = 16
F32 = jnp.float32
BF16 = jnp.bfloat16


def exchange_kernel(tm_count, n, x_ref, r_ref, send_sem, recv_sem, send_next, recv_prev, own_sem):
    tm = lax.axis_index("tm")
    me = lax.axis_index("space")
    barrier = pltpu.get_barrier_semaphore()

    @pl.loop(1, n)
    def _(k):
        pl.semaphore_signal(barrier, inc=1, device_id=(tm, lax.rem(me + k, n)), device_id_type=MESH)

    @pl.when(tm > 0)
    def _():
        @pl.loop(0, n)
        def _(k):
            pl.semaphore_signal(barrier, inc=1, device_id=(tm - 1, lax.rem(me + k, n)), device_id_type=MESH)

    own = pltpu.make_async_copy(x_ref.at[pl.ds(me, 3)], r_ref.at[1, me], own_sem)
    own.start()

    @pl.when(tm == 0)
    def _():
        r_ref[0] = jnp.zeros(r_ref.shape[1:], r_ref.dtype)

    pl.semaphore_wait(barrier, n - 1 + n * (1 - tm // (tm_count - 1)))

    @pl.when(tm < tm_count - 1)
    def _():
        @pl.loop(0, n)
        def _(k):
            to = lax.rem(me + k, n)
            pltpu.make_async_remote_copy(
                src_ref=x_ref.at[pl.ds(to, 3)], dst_ref=r_ref.at[0, me],
                send_sem=send_next, recv_sem=recv_prev,
                device_id=(tm + 1, to), device_id_type=MESH,
            ).start()

    @pl.loop(1, n)
    def _(k):
        to = lax.rem(me + k, n)
        pltpu.make_async_remote_copy(
            src_ref=x_ref.at[pl.ds(to, 3)], dst_ref=r_ref.at[1, me],
            send_sem=send_sem, recv_sem=recv_sem,
            device_id=(tm, to), device_id_type=MESH,
        ).start()

    def await_all(half, count, sem):
        whole = r_ref.at[half, pl.ds(0, count)]
        pltpu.make_async_copy(whole, whole, sem).wait()

    own.wait()
    await_all(1, n - 1, send_sem)
    await_all(1, n - 1, recv_sem)

    @pl.when(tm < tm_count - 1)
    def _():
        await_all(0, n, send_next)

    @pl.when(tm > 0)
    def _():
        await_all(0, n, recv_prev)


def exchange(x, tm_count, n):
    return pl.pallas_call(
        functools.partial(exchange_kernel, tm_count, n),
        out_shape=jax.ShapeDtypeStruct((2, n, 3) + x.shape[1:], x.dtype),
        in_specs=[pl.BlockSpec(memory_space=pltpu.VMEM)],
        out_specs=pl.BlockSpec(memory_space=pltpu.VMEM),
        scratch_shapes=[pltpu.SemaphoreType.DMA] * 5,
        compiler_params=pltpu.CompilerParams(collective_id=0, has_side_effects=True),
        name="exchange",
    )(x)


def block_kernel(tm_count, n, g_ref, win_ref, bin_ref, gain_ref, w_ref, bmid_ref, out_ref, act, feat, tmp):
    cols = 64
    first_frames = lax.axis_index("tm") == 0
    me = lax.axis_index("space")
    bias = bin_ref[...]
    gain = gain_ref[...]
    for pair in range(2):
        lanes = slice(128 * pair, 128 * pair + 256)
        left = jnp.concatenate([g_ref[cols * a : cols * a + 6 * cols, lanes] for a in range(3)], axis=1)
        for row in range(2):
            rho = 2 * pair + row
            both = jnp.dot(left, win_ref[:, 2 * C * row : 2 * C * (row + 1)], preferred_element_type=F32)
            inside = True
            if rho == 0:
                inside = me > 0
            if rho == 3:
                inside = me < n - 1
            for parity in range(2):
                f = (both[:, C * parity : C * (parity + 1)] + bias).astype(BF16)
                if rho in (1, 2):
                    for frame in range(4):
                        feat[frame, rho - 1, parity] = f[cols * (frame + 2) : cols * (frame + 3)]
                v = f.astype(F32)
                scale = lax.rsqrt(jnp.mean(v * v, axis=-1, keepdims=True) + 1e-6)
                h = v * scale * (0.5 * gain)
                s = (h + h * jnp.tanh(h)).astype(BF16)
                for frame in range(6):
                    piece = s[cols * frame : cols * (frame + 1)]
                    keep = inside
                    if frame < 2:
                        keep = jnp.logical_and(keep, jnp.logical_not(first_frames))
                    if keep is not True:
                        piece = jnp.where(keep, piece, jnp.zeros_like(piece))
                    act[frame, rho, parity] = piece

    bmid = bmid_ref[...]

    @pl.loop(0, 4)
    def _(frame):
        lefts, rights = [], []
        for a in range(3):
            for b in range(3):
                lefts.append(act[frame + a, b : b + 2].reshape(4 * cols, C))
                rights.append(jnp.concatenate([w_ref[a, b, e] for e in range(3)], axis=1))
        sums = jnp.dot(
            jnp.concatenate(lefts, axis=1), jnp.concatenate(rights, axis=0), preferred_element_type=F32
        )
        edge = lax.broadcasted_iota(jnp.int32, (cols, C), 0)
        for y in range(2):
            even_in = sums[128 * y : 128 * y + 64]
            odd_in = sums[128 * y + 64 : 128 * y + 128]
            down = jnp.where(edge == 0, 0.0, pltpu.roll(odd_in[:, :C], 1, 0))
            up = jnp.where(edge == cols - 1, 0.0, pltpu.roll(even_in[:, 2 * C :], cols - 1, 0))
            even = down + even_in[:, C : 2 * C] + odd_in[:, 2 * C :]
            odd = even_in[:, :C] + odd_in[:, C : 2 * C] + up
            even = feat[frame, y, 0].astype(F32) + even + bmid
            odd = feat[frame, y, 1].astype(F32) + odd + bmid
            for k in range(3):
                ln = slice(128 * k, 128 * (k + 1))
                tmp[y, k, pl.ds(0, 64, stride=2), :] = even[:, ln]
                tmp[y, k, pl.ds(1, 64, stride=2), :] = odd[:, ln]
            for k in range(3):
                ln = slice(128 * k, 128 * (k + 1))
                out_ref[frame, y, :, ln] = tmp[y, k].astype(BF16)


def block(g, win, bin_, gain, w, bmid, tm_count, n):
    vm = pl.BlockSpec(memory_space=pltpu.VMEM)
    return pl.pallas_call(
        functools.partial(block_kernel, tm_count, n),
        out_shape=jax.ShapeDtypeStruct((4, 2, 128, C), BF16),
        in_specs=[vm] * 6,
        out_specs=vm,
        scratch_shapes=[
            pltpu.VMEM((6, 4, 2, 64, C), BF16),
            pltpu.VMEM((4, 2, 2, 64, C), BF16),
            pltpu.VMEM((2, 3, 128, 128), F32),
        ],
        compiler_params=pltpu.CompilerParams(vmem_limit_bytes=56 << 20),
        name="block",
    )(g, win, bin_, gain, w, bmid)


def spread_weight(w):
    zero = jnp.zeros_like(w)
    cols = jnp.concatenate([w, zero[:, :, :1]], 2), jnp.concatenate([zero[:, :, :1], w], 2)
    both = jnp.stack(cols, axis=4)
    pad = jnp.zeros_like(both[:, :1])
    rows = jnp.stack([jnp.concatenate([both, pad], 1), jnp.concatenate([pad, both], 1)], axis=4)
    return rows.reshape(3 * 4 * 4 * LAT, 4 * C)


def gather_columns(r):
    two, n, three = r.shape[:3]
    t = r.reshape(two, n, three, 2, 2, 2, 2, LAT).transpose(0, 3, 4, 1, 2, 5, 6, 7)
    t = t.reshape(8, n, 6, 2, LAT)
    before = jnp.pad(t[:, :-1, :, 1:], ((0, 0), (1, 0), (0, 0), (0, 0), (0, 0)))
    after = jnp.pad(t[:, 1:, :, :1], ((0, 0), (0, 1), (0, 0), (0, 0), (0, 0)))
    return jnp.concatenate([before, t, after], axis=3).reshape(8 * n, 6 * 4 * LAT)


def solution(mesh):
    tm_count, n = mesh.shape["tm"], mesh.shape["space"]

    def per_device(tokens, w_in, b_in, gain, w_mid, b_mid):
        x = tokens[:, :, 0].transpose(1, 0, 2).reshape(n, 2, 128)
        x = jnp.pad(x, ((1, 1), (0, 0), (0, 0)))
        r = exchange(x, tm_count, n)
        g = gather_columns(r)
        row = lambda v: v.reshape(1, C)
        return block(g, spread_weight(w_in), row(b_in), row(gain), w_mid, row(b_mid), tm_count, n)

    return jax.shard_map(
        per_device,
        mesh=mesh,
        in_specs=(P("tm", None, "space", None), P(), P(), P(), P(), P()),
        out_specs=P("tm", "space", None, None),
        check_vma=False,
    )
```

```python
import functools

import jax
import jax.numpy as jnp
from jax import lax
from jax.experimental import pallas as pl
from jax.experimental.pallas import tpu as pltpu
from jax.sharding import PartitionSpec as P

MESH = pl.DeviceIdType.MESH
C = 384
LAT = 16
COLS = 64
F32 = jnp.float32
BF16 = jnp.bfloat16
SPACE = (2, 4, 8)


def far_first():
    def hops(step):
        return sum(min(d, size - d) for d, size in zip(step, SPACE))

    steps = [(i, j, k) for i in range(SPACE[0]) for j in range(SPACE[1]) for k in range(SPACE[2])]
    return sorted(steps, key=hops, reverse=True)


def exchange_kernel(
    tm_count, n, tok_hbm, w_in_hbm, w_hbm, r_ref, win_ref, pick_ref, w_ref, u_ref,
    tok, x, w_in, send_sem, recv_sem, send_next, recv_prev, own_sem, tok_sem, w_in_sem, w_sem,
):
    tm = lax.axis_index("tm")
    me = lax.axis_index("space")
    copies = (
        pltpu.make_async_copy(tok_hbm, tok, tok_sem),
        pltpu.make_async_copy(w_in_hbm, w_in, w_in_sem),
        pltpu.make_async_copy(w_hbm, w_ref, w_sem),
    )
    for copy in copies:
        copy.start()

    _, ny, nz = SPACE
    place = (me // (ny * nz), (me // nz) % ny, me % nz)
    strides = (ny * nz, nz, 1)
    along = [[((place[d] + s) % SPACE[d]) * strides[d] for s in range(SPACE[d])] for d in range(3)]
    peers = [along[0][i] + along[1][j] + along[2][k] for i, j, k in far_first()]

    barrier = pltpu.get_barrier_semaphore()

    @pl.when(tm > 0)
    def _():
        for peer in peers:
            pl.semaphore_signal(barrier, inc=1, device_id=(tm - 1, peer), device_id_type=MESH)

    copies[0].wait()
    for h in range(2):
        x[:, h, :] = jnp.concatenate([tok[2 * h], tok[2 * h + 1]], axis=1)

    for peer in peers[:-1]:
        pl.semaphore_signal(barrier, inc=1, device_id=(tm, peer), device_id_type=MESH)

    @pl.when(tm == 0)
    def _():
        r_ref[0] = jnp.zeros(r_ref.shape[1:], r_ref.dtype)

    def rows_for(peer):
        return x.at[pl.ds(jnp.clip(peer - 1, 0, n - 3), 3)]

    pl.semaphore_wait(barrier, n - 1 + n * (1 - tm // (tm_count - 1)))
    own = pltpu.make_async_copy(rows_for(me), r_ref.at[1, me], own_sem)
    own.start()

    @pl.when(tm < tm_count - 1)
    def _():
        for peer in peers:
            pltpu.make_async_remote_copy(
                src_ref=rows_for(peer), dst_ref=r_ref.at[0, me], send_sem=send_next, recv_sem=recv_prev,
                device_id=(tm + 1, peer), device_id_type=MESH,
            ).start()

    for peer in peers[:-1]:
        pltpu.make_async_remote_copy(
            src_ref=rows_for(peer), dst_ref=r_ref.at[1, me], send_sem=send_sem, recv_sem=recv_sem,
            device_id=(tm, peer), device_id_type=MESH,
        ).start()

    copies[1].wait()
    win_ref[...] = jnp.zeros(win_ref.shape, BF16)
    for a in range(3):
        for b in range(3):
            block = w_in[a, b].reshape(3 * LAT, C)
            for row in range(2):
                for parity in range(2):
                    start = ((a * 4 + b + row) * 4 + parity) * LAT
                    lanes = slice((2 * row + parity) * C, (2 * row + parity + 1) * C)
                    win_ref[start : start + 3 * LAT, lanes] = block

    lane = lax.broadcasted_iota(jnp.int32, (C, C), 1)
    have = lax.broadcasted_iota(jnp.int32, (C, C), 0)
    y, col, c = lane // 64, (lane // 16) % 4, lane % 16
    shift = jnp.where(me == 0, -1, jnp.where(me == n - 1, 1, 0))
    want = (y // 2 + shift) * 128 + (y % 2) * 32 + ((col + 1) % 2) * 16 + c
    for fp in range(2):
        pick_ref[:, C * fp : C * (fp + 1)] = jnp.where(have == want + 64 * fp, 1.0, 0.0).astype(BF16)

    copies[2].wait()

    @pl.loop(0, 9)
    def _(i):
        a, e = i // 3, i % 3
        for part in range(3):
            rows = slice(128 * part, 128 * (part + 1))
            outer = 0.5 * (w_ref[a, 0, e, rows].astype(F32) + w_ref[a, 2, e, rows].astype(F32))
            inner = 0.5 * w_ref[a, 1, e, rows].astype(F32)
            u_ref[0, a, e, rows] = (outer + inner).astype(BF16)
            u_ref[1, a, e, rows] = (outer - inner).astype(BF16)

    def await_all(half, count, sem):
        whole = r_ref.at[half, pl.ds(0, count)]
        pltpu.make_async_copy(whole, whole, sem).wait()

    own.wait()
    await_all(1, n - 1, send_sem)
    await_all(1, n - 1, recv_sem)

    @pl.when(tm < tm_count - 1)
    def _():
        await_all(0, n, send_next)

    @pl.when(tm > 0)
    def _():
        await_all(0, n, recv_prev)


def exchange(tok, w_in, w, tm_count, n):
    hbm = pl.BlockSpec(memory_space=pltpu.HBM)
    vm = pl.BlockSpec(memory_space=pltpu.VMEM)
    return pl.pallas_call(
        functools.partial(exchange_kernel, tm_count, n),
        out_shape=(
            jax.ShapeDtypeStruct((2, n, 3, 2, 128), BF16),
            jax.ShapeDtypeStruct((3 * 4 * 4 * LAT, 4 * C), BF16),
            jax.ShapeDtypeStruct((C, 2 * C), BF16),
            jax.ShapeDtypeStruct(w.shape, BF16),
            jax.ShapeDtypeStruct((2, 3, 3, C, C), BF16),
        ),
        in_specs=[hbm] * 3,
        out_specs=[vm] * 5,
        scratch_shapes=[
            pltpu.VMEM(tok.shape, BF16),
            pltpu.VMEM((n, 2, 128), BF16),
            pltpu.VMEM(w_in.shape, BF16),
        ]
        + [pltpu.SemaphoreType.DMA] * 8,
        compiler_params=pltpu.CompilerParams(collective_id=0, has_side_effects=True, vmem_limit_bytes=24 << 20),
        name="exchange",
    )(*(pltpu.with_memory_space_constraint(v, pltpu.HBM) for v in (tok, w_in, w)))


def block_kernel(
    tm_count, n, r_ref, win_ref, pick_ref, w_ref, u_ref, bin_ref, gain_ref, bmid_ref, out_ref, g, act, d, feat, part, tmp
):
    first_frames = lax.axis_index("tm") == 0
    me = lax.axis_index("space")

    sub = lax.broadcasted_iota(jnp.int32, (COLS, C), 0)
    col = (lax.broadcasted_iota(jnp.int32, (COLS, C), 1) // 16) % 4
    came = jnp.concatenate(
        [
            jnp.concatenate([r_ref[tb, :, t, h, :] for t in range(3)], axis=1)
            for tb in range(2)
            for h in range(2)
        ],
        axis=0,
    )
    laid = jnp.dot(came, pick_ref[...], preferred_element_type=F32)
    for k in range(4):
        for fp in range(2):
            here = laid[COLS * k : COLS * (k + 1), C * fp : C * (fp + 1)]
            before = jnp.where(sub == 0, 0.0, pltpu.roll(here, 1, 0))
            after = jnp.where(sub == COLS - 1, 0.0, pltpu.roll(here, COLS - 1, 0))
            g[2 * k + fp] = jnp.where(col == 0, before, jnp.where(col == 3, after, here)).astype(BF16)

    bias = bin_ref[...].reshape(1, C)
    half_gain = 0.5 * gain_ref[...].reshape(1, C)
    for pair in range(2):
        lanes = slice(128 * pair, 128 * pair + 256)
        left = jnp.concatenate([g[a : a + 6, :, lanes].reshape(6 * COLS, 256) for a in range(3)], axis=1)
        rows = []
        for row in range(2):
            rho = 2 * pair + row
            both = jnp.dot(left, win_ref[:, 2 * C * row : 2 * C * (row + 1)], preferred_element_type=F32)
            inside = True
            if rho == 0:
                inside = me > 0
            if rho == 3:
                inside = me < n - 1
            for parity in range(2):
                for frame in range(6):
                    f = both[COLS * frame : COLS * (frame + 1), C * parity : C * (parity + 1)]
                    f = (f + bias).astype(BF16)
                    if rho in (1, 2) and frame >= 2:
                        feat[frame - 2, rho - 1, parity] = f
                    v = f.astype(F32)
                    scale = lax.rsqrt(jnp.mean(v * v, axis=-1, keepdims=True) + 1e-6)
                    half = v * scale * half_gain
                    s = half + half * jnp.tanh(half)
                    keep = inside
                    if frame < 2:
                        keep = jnp.logical_and(keep, jnp.logical_not(first_frames))
                    if keep is not True:
                        s = jnp.where(keep, s, 0.0)
                    s = s.astype(BF16)
                    at = pl.ds(128 * frame + COLS * parity, COLS)
                    if rho < 2:
                        act[rho, frame, parity] = s
                    elif rho == 2:
                        a0 = act[0, frame, parity].astype(F32)
                        a1 = act[1, frame, parity].astype(F32)
                        s = s.astype(F32)
                        d[0, at] = (a0 - s).astype(BF16)
                        d[1, at] = (a1 + s).astype(BF16)
                        d[2, at] = (s - a1).astype(BF16)
                    else:
                        a1 = act[1, frame, parity].astype(F32)
                        d[3, at] = (a1 - s.astype(F32)).astype(BF16)

    bmid = bmid_ref[...].reshape(1, C)
    edge = lax.broadcasted_iota(jnp.int32, (COLS, 128), 0)
    cells = [(k, e) for k in range(3) for e in range(3)]

    def weight(eta, a, k, e):
        lanes = slice(128 * k, 128 * (k + 1))
        if eta == 0:
            return w_ref[a, 0, e, :, lanes]
        if eta == 3:
            return w_ref[a, 2, e, :, lanes]
        return u_ref[eta - 1, a, e, :, lanes]

    done = 0
    for tile in range(5):
        here = cells[2 * tile : 2 * tile + 2]
        m = []
        for eta in range(4):
            left = jnp.concatenate([d[eta, 128 * a : 128 * a + 512] for a in range(3)], axis=1)
            right = jnp.concatenate(
                [jnp.concatenate([weight(eta, a, k, e) for k, e in here], axis=1) for a in range(3)], axis=0
            )
            m.append(jnp.dot(left, right, preferred_element_type=F32))
        lanes = slice(256 * tile, 256 * tile + 128 * len(here))
        part[0, :, lanes] = (m[1] + m[2]) + m[0]
        part[1, :, lanes] = (m[1] - m[2]) - m[3]
        while done < 3 and 3 * (done + 1) <= 2 * tile + len(here):
            k = done
            done += 1
            ln = slice(128 * k, 128 * (k + 1))
            by_tap = [slice(128 * (3 * k + e), 128 * (3 * k + e + 1)) for e in range(3)]
            for frame in range(4):
                at_even = slice(128 * frame, 128 * frame + COLS)
                at_odd = slice(128 * frame + COLS, 128 * (frame + 1))
                for yy in range(2):
                    down = jnp.where(edge == 0, 0.0, pltpu.roll(part[yy, at_odd, by_tap[0]], 1, 0))
                    up = jnp.where(edge == COLS - 1, 0.0, pltpu.roll(part[yy, at_even, by_tap[2]], COLS - 1, 0))
                    even = down + part[yy, at_even, by_tap[1]] + part[yy, at_odd, by_tap[2]]
                    odd = part[yy, at_even, by_tap[0]] + part[yy, at_odd, by_tap[1]] + up
                    even = feat[frame, yy, 0, :, ln].astype(F32) + even + bmid[:, ln]
                    odd = feat[frame, yy, 1, :, ln].astype(F32) + odd + bmid[:, ln]
                    tmp[k, frame, yy, pl.ds(0, COLS, stride=2), :] = even
                    tmp[k, frame, yy, pl.ds(1, COLS, stride=2), :] = odd
                    out_ref[frame, yy, :, ln] = tmp[k, frame, yy].astype(BF16)


def block(r, win, pick, w, u, b_in, gain, b_mid, tm_count, n):
    vm = pl.BlockSpec(memory_space=pltpu.VMEM)
    return pl.pallas_call(
        functools.partial(block_kernel, tm_count, n),
        out_shape=jax.ShapeDtypeStruct((4, 2, 2 * COLS, C), BF16),
        in_specs=[vm] * 8,
        out_specs=vm,
        scratch_shapes=[
            pltpu.VMEM((8, COLS, C), BF16),
            pltpu.VMEM((2, 6, 2, COLS, C), BF16),
            pltpu.VMEM((4, 6 * 128, C), BF16),
            pltpu.VMEM((4, 2, 2, COLS, C), BF16),
            pltpu.VMEM((2, 512, 3 * C), F32),
            pltpu.VMEM((3, 4, 2, 128, 128), F32),
        ],
        compiler_params=pltpu.CompilerParams(vmem_limit_bytes=24 << 20),
        name="block",
    )(r, win, pick, w, u, b_in, gain, b_mid)


def solution(mesh):
    tm_count, n = mesh.shape["tm"], mesh.shape["space"]

    def per_device(tokens, w_in, b_in, gain, w_mid, b_mid):
        r, win, pick, w, u = exchange(tokens[:, :, 0], w_in, w_mid, tm_count, n)
        return block(r, win, pick, w, u, b_in, gain, b_mid, tm_count, n)

    return jax.shard_map(
        per_device,
        mesh=mesh,
        in_specs=(P("tm", None, "space", None), P(), P(), P(), P(), P()),
        out_specs=P("tm", "space", None, None),
        check_vma=False,
    )
```

```python
import functools

import jax
import jax.numpy as jnp
from jax import lax
from jax.experimental import pallas as pl
from jax.experimental.pallas import tpu as pltpu
from jax.sharding import PartitionSpec as P

MESH = pl.DeviceIdType.MESH
C = 384
LAT = 16
COLS = 64
F32 = jnp.float32
BF16 = jnp.bfloat16
SPACE = (2, 4, 8)


def far_first():
    def hops(step):
        return sum(min(d, size - d) for d, size in zip(step, SPACE))

    steps = [(i, j, k) for i in range(SPACE[0]) for j in range(SPACE[1]) for k in range(SPACE[2])]
    return sorted(steps, key=hops, reverse=True)


def lay_out_columns(r_ref, tb, pick_ref, spread, g, first):
    came = jnp.concatenate([r_ref[tb, t].reshape(2 * COLS, 128) for t in range(3)], axis=1)
    laid = jnp.dot(came, pick_ref[...], preferred_element_type=F32)
    spread[:, 0:8, :] = jnp.zeros((6, 8, 128), F32)
    spread[:, 136:144, :] = jnp.zeros((6, 8, 128), F32)
    for k in range(6):
        spread[k, 8:136, :] = laid[:, 128 * k : 128 * (k + 1)]
    col = (lax.broadcasted_iota(jnp.int32, (COLS, 128), 1) // 16) % 4
    for h in range(2):
        for fp in range(2):
            for q in range(3):
                before, here, after = (
                    spread[3 * fp + q, pl.ds(8 + h + 2 * step, COLS, stride=2), :] for step in (-1, 0, 1)
                )
                both = jnp.where(col == 0, before, jnp.where(col == 3, after, here))
                g[first + 2 * h + fp, :, 128 * q : 128 * (q + 1)] = both.astype(BF16)


def first_products(frames, count, win_ref):
    both = []
    for pair in range(2):
        lanes = slice(128 * pair, 128 * pair + 256)
        left = jnp.concatenate([frames(a, lanes) for a in range(3)], axis=1)
        for row in range(2):
            both.append(
                jnp.dot(left, win_ref[:, 2 * C * row : 2 * C * (row + 1)], preferred_element_type=F32)
            )
    return both


def activate(both, sub, bias, half_gain, keeps, feat, d):
    for parity in range(2):
        for block_row in range(COLS // 16):
            rows = slice(COLS * sub + 16 * block_row, COLS * sub + 16 * (block_row + 1))
            s = []
            for rho in range(4):
                f = (both[rho][rows, C * parity : C * (parity + 1)] + bias).astype(BF16)
                if rho in (1, 2) and feat is not None:
                    feat[rho - 1, parity, 16 * block_row : 16 * (block_row + 1)] = f
                v = f.astype(F32)
                scale = lax.rsqrt(jnp.sum(v * v, axis=-1, keepdims=True) * (1.0 / C) + 1e-6)
                if keeps[rho] is not None:
                    scale = scale * keeps[rho]
                half = v * scale * half_gain
                s.append(half + half * jnp.tanh(half))
            start = 128 * sub + COLS * parity + 16 * block_row
            at = slice(start, start + 16)
            d[0, at] = (s[0] - s[2]).astype(BF16)
            d[1, at] = (s[1] + s[2]).astype(BF16)
            d[2, at] = (s[2] - s[1]).astype(BF16)
            d[3, at] = (s[1] - s[3]).astype(BF16)


def edges(n):
    me = lax.axis_index("space")
    return jnp.where(me == 0, 0.0, 1.0), None, None, jnp.where(me == n - 1, 0.0, 1.0)


def exchange_kernel(
    tm_count, n, tok_hbm, w_in_hbm, w_hbm, bin_hbm, gain_hbm,
    r_ref, win_ref, pick_ref, w_ref, u_ref, g_ref, feat_ref, d_ref,
    tok, x, w_in, bin_ref, gain_ref, spread,
    send_sem, recv_sem, send_next, recv_prev, own_sem, tok_sem, w_in_sem, bin_sem, gain_sem, w_sem,
):
    tm = lax.axis_index("tm")
    me = lax.axis_index("space")
    copies = (
        pltpu.make_async_copy(tok_hbm, tok, tok_sem),
        pltpu.make_async_copy(w_in_hbm, w_in, w_in_sem),
        pltpu.make_async_copy(bin_hbm, bin_ref, bin_sem),
        pltpu.make_async_copy(gain_hbm, gain_ref, gain_sem),
        pltpu.make_async_copy(w_hbm, w_ref, w_sem),
    )
    for copy in copies:
        copy.start()

    _, ny, nz = SPACE
    place = (me // (ny * nz), (me // nz) % ny, me % nz)
    strides = (ny * nz, nz, 1)
    along = [[((place[d] + s) % SPACE[d]) * strides[d] for s in range(SPACE[d])] for d in range(3)]
    peers = [along[0][i] + along[1][j] + along[2][k] for i, j, k in far_first()]

    barrier = pltpu.get_barrier_semaphore()

    def signal(group):
        for peer in group:
            if peer is not peers[-1]:
                pl.semaphore_signal(barrier, inc=1, device_id=(tm, peer), device_id_type=MESH)

        @pl.when(tm > 0)
        def _():
            for peer in group:
                pl.semaphore_signal(barrier, inc=1, device_id=(tm - 1, peer), device_id_type=MESH)

    signal(peers[:40])
    copies[0].wait()
    for h in range(2):
        x[:, h, :] = jnp.concatenate([tok[2 * h], tok[2 * h + 1]], axis=1)
    signal(peers[40:])

    @pl.when(tm == 0)
    def _():
        r_ref[0] = jnp.zeros(r_ref.shape[1:], r_ref.dtype)

    def rows_for(peer):
        return x.at[pl.ds(jnp.clip(peer - 1, 0, n - 3), 3)]

    pl.semaphore_wait(barrier, n - 1 + n * (1 - tm // (tm_count - 1)))
    own = pltpu.make_async_copy(rows_for(me), r_ref.at[1, :, me], own_sem)
    own.start()

    for peer in peers[:-1]:
        pltpu.make_async_remote_copy(
            src_ref=rows_for(peer), dst_ref=r_ref.at[1, :, me], send_sem=send_sem, recv_sem=recv_sem,
            device_id=(tm, peer), device_id_type=MESH,
        ).start()

    @pl.when(tm < tm_count - 1)
    def _():
        for peer in peers:
            pltpu.make_async_remote_copy(
                src_ref=rows_for(peer), dst_ref=r_ref.at[0, :, me], send_sem=send_next, recv_sem=recv_prev,
                device_id=(tm + 1, peer), device_id_type=MESH,
            ).start()

    copies[1].wait()
    win_ref[...] = jnp.zeros(win_ref.shape, BF16)
    for a in range(3):
        for b in range(3):
            block = w_in[a, b].reshape(3 * LAT, C)
            for row in range(2):
                for parity in range(2):
                    start = ((a * 4 + b + row) * 4 + parity) * LAT
                    lanes = slice((2 * row + parity) * C, (2 * row + parity + 1) * C)
                    win_ref[start : start + 3 * LAT, lanes] = block

    lane = lax.broadcasted_iota(jnp.int32, (C, C), 1)
    have = lax.broadcasted_iota(jnp.int32, (C, C), 0)
    y, col, c = lane // 64, (lane // 16) % 4, lane % 16
    shift = jnp.where(me == 0, -1, jnp.where(me == n - 1, 1, 0))
    want = (y // 2 + shift) * 128 + (y % 2) * 32 + ((col + 1) % 2) * 16 + c
    for fp in range(2):
        pick_ref[:, C * fp : C * (fp + 1)] = jnp.where(have == want + 64 * fp, 1.0, 0.0).astype(BF16)

    copies[4].wait()

    @pl.loop(0, 9)
    def _(i):
        a, e = i // 3, i % 3
        for part in range(3):
            rows = slice(128 * part, 128 * (part + 1))
            outer = 0.5 * (w_ref[a, 0, e, rows].astype(F32) + w_ref[a, 2, e, rows].astype(F32))
            inner = 0.5 * w_ref[a, 1, e, rows].astype(F32)
            u_ref[0, a, e, rows] = (outer + inner).astype(BF16)
            u_ref[1, a, e, rows] = (outer - inner).astype(BF16)

    def await_all(half, count, sem):
        whole = r_ref.at[half, :, pl.ds(0, count)]
        pltpu.make_async_copy(whole, whole, sem).wait()

    own.wait()
    await_all(1, n - 1, recv_sem)

    copies[2].wait()
    copies[3].wait()
    lay_out_columns(r_ref, 1, pick_ref, spread, g_ref, 0)
    both = first_products(
        lambda a, lanes: g_ref[a : a + 2, :, lanes].reshape(2 * COLS, 256), 2, win_ref
    )
    bias = bin_ref[...].reshape(1, C)
    half_gain = 0.5 * gain_ref[...].reshape(1, C)
    for sub in range(2):
        activate(both, sub, bias, half_gain, edges(n), feat_ref.at[sub], d_ref)

    await_all(1, n - 1, send_sem)

    @pl.when(tm < tm_count - 1)
    def _():
        await_all(0, n, send_next)

    @pl.when(tm > 0)
    def _():
        await_all(0, n, recv_prev)


def exchange(tok, w_in, w, b_in, gain, tm_count, n):
    hbm = pl.BlockSpec(memory_space=pltpu.HBM)
    vm = pl.BlockSpec(memory_space=pltpu.VMEM)
    return pl.pallas_call(
        functools.partial(exchange_kernel, tm_count, n),
        out_shape=(
            jax.ShapeDtypeStruct((2, 3, n, 2, 128), BF16),
            jax.ShapeDtypeStruct((3 * 4 * 4 * LAT, 4 * C), BF16),
            jax.ShapeDtypeStruct((C, 2 * C), BF16),
            jax.ShapeDtypeStruct(w.shape, BF16),
            jax.ShapeDtypeStruct((2, 3, 3, C, C), BF16),
            jax.ShapeDtypeStruct((4, COLS, C), BF16),
            jax.ShapeDtypeStruct((2, 2, 2, COLS, C), BF16),
            jax.ShapeDtypeStruct((4, 2 * 128, C), BF16),
        ),
        in_specs=[hbm] * 5,
        out_specs=[vm] * 8,
        scratch_shapes=[
            pltpu.VMEM(tok.shape, BF16),
            pltpu.VMEM((n, 2, 128), BF16),
            pltpu.VMEM(w_in.shape, BF16),
            pltpu.VMEM((C,), F32),
            pltpu.VMEM((C,), F32),
            pltpu.VMEM((6, 2 * COLS + 16, 128), F32),
        ]
        + [pltpu.SemaphoreType.DMA] * 10,
        compiler_params=pltpu.CompilerParams(collective_id=0, has_side_effects=True, vmem_limit_bytes=24 << 20),
        name="exchange",
    )(*(pltpu.with_memory_space_constraint(v, pltpu.HBM) for v in (tok, w_in, w, b_in, gain)))


def block_kernel(
    tm_count, n, r_ref, win_ref, pick_ref, w_ref, u_ref, own_g, own_feat, own_d, bin_ref, gain_ref, bmid_ref,
    out_ref, spread, g, d, feat, part, down, up, tmp, made, out_sem,
):
    down[:, :, :, 0:8, :] = jnp.zeros(down.shape[:3] + (8, 128), F32)
    up[:, :, :, COLS : COLS + 8, :] = jnp.zeros(up.shape[:3] + (8, 128), F32)
    lay_out_columns(r_ref, 0, pick_ref, spread, g, 0)

    def frames(first, lanes):
        before = [g[first:4, :, lanes].reshape((4 - first) * COLS, 256)]
        if first:
            before.append(own_g[0:first, :, lanes].reshape(first * COLS, 256))
        return jnp.concatenate(before, axis=0)

    both = first_products(frames, 4, win_ref)
    bias = bin_ref[...].reshape(1, C)
    half_gain = 0.5 * gain_ref[...].reshape(1, C)
    not_first = jnp.where(lax.axis_index("tm") == 0, 0.0, 1.0)
    inside = edges(n)
    early = [not_first if keep is None else keep * not_first for keep in inside]
    for frame in range(4):
        activate(
            both, frame, bias, half_gain, early if frame < 2 else inside, feat.at[frame - 2] if frame >= 2 else None, d
        )

    bmid = bmid_ref[...].reshape(1, C)
    cells = [(k, e) for k in range(3) for e in range(3)]

    def weight(eta, a, k, e):
        lanes = slice(128 * k, 128 * (k + 1))
        if eta == 0:
            return w_ref[a, 0, e, :, lanes]
        if eta == 3:
            return w_ref[a, 2, e, :, lanes]
        return u_ref[eta - 1, a, e, :, lanes]

    def window(eta, a):
        rows = [d[eta, 128 * a : 512]]
        if a:
            rows.append(own_d[eta, 0 : 128 * a])
        return jnp.concatenate(rows, axis=0)

    def mix(tile):
        here = cells[2 * tile : 2 * tile + 2]
        m = []
        for eta in range(4):
            left = jnp.concatenate([window(eta, a) for a in range(3)], axis=1)
            right = jnp.concatenate(
                [jnp.concatenate([weight(eta, a, k, e) for k, e in here], axis=1) for a in range(3)], axis=0
            )
            m.append(jnp.dot(left, right, preferred_element_type=F32))
        total = ((m[1] + m[2]) + m[0], (m[1] - m[2]) - m[3])
        for place, (k, e) in enumerate(here):
            for y in range(2):
                mine = total[y][:, 128 * place : 128 * (place + 1)]
                for frame in range(4):
                    even = mine[128 * frame : 128 * frame + COLS]
                    odd = mine[128 * frame + COLS : 128 * (frame + 1)]
                    if e == 2:
                        up[y, k, frame, 0:COLS, :] = even
                    else:
                        part[y, 3 * k + e, 128 * frame : 128 * frame + COLS] = even
                    if e == 0:
                        down[y, k, frame, 8 : 8 + COLS, :] = odd
                    else:
                        part[y, 3 * k + e, 128 * frame + COLS : 128 * (frame + 1)] = odd

    def out_copy(k):
        at = (slice(None), slice(None), slice(None), slice(128 * k, 128 * (k + 1)))
        return pltpu.make_async_copy(made.at[at], out_ref.at[at], out_sem.at[k])

    def finish(k):
        ln = slice(128 * k, 128 * (k + 1))
        for frame in range(4):
            even_rows = slice(128 * frame, 128 * frame + COLS)
            odd_rows = slice(128 * frame + COLS, 128 * (frame + 1))
            have = feat.at[frame] if frame < 2 else own_feat.at[frame - 2]
            for y in range(2):
                even = down[y, k, frame, pl.ds(7, COLS), :] + part[y, 3 * k + 1, even_rows] + part[y, 3 * k + 2, odd_rows]
                odd = part[y, 3 * k, even_rows] + part[y, 3 * k + 1, odd_rows] + up[y, k, frame, pl.ds(1, COLS), :]
                even = have[y, 0, :, ln].astype(F32) + even + bmid[:, ln]
                odd = have[y, 1, :, ln].astype(F32) + odd + bmid[:, ln]
                slot = tmp.at[k, frame, y]
                slot[pl.ds(0, COLS, stride=2), :] = even
                slot[pl.ds(1, COLS, stride=2), :] = odd
                made[frame, y, :, ln] = slot[...].astype(BF16)
        out_copy(k).start()

    mix(0)
    mix(1)
    finish(0)
    mix(2)
    finish(1)
    mix(3)
    mix(4)
    finish(2)
    for k in range(3):
        out_copy(k).wait()


def block(r, win, pick, w, u, own_g, own_feat, own_d, b_in, gain, b_mid, tm_count, n):
    vm = pl.BlockSpec(memory_space=pltpu.VMEM)
    return pl.pallas_call(
        functools.partial(block_kernel, tm_count, n),
        out_shape=jax.ShapeDtypeStruct((4, 2, 2 * COLS, C), BF16),
        in_specs=[vm] * 11,
        out_specs=pl.BlockSpec(memory_space=pl.ANY),
        scratch_shapes=[
            pltpu.VMEM((6, 2 * COLS + 16, 128), F32),
            pltpu.VMEM((4, COLS, C), BF16),
            pltpu.VMEM((4, 4 * 128, C), BF16),
            pltpu.VMEM((2, 2, 2, COLS, C), BF16),
            pltpu.VMEM((2, 9, 512, 128), F32),
            pltpu.VMEM((2, 3, 4, COLS + 8, 128), F32),
            pltpu.VMEM((2, 3, 4, COLS + 8, 128), F32),
            pltpu.VMEM((3, 4, 2, 128, 128), F32),
            pltpu.VMEM((4, 2, 2 * COLS, C), BF16),
            pltpu.SemaphoreType.DMA((3,)),
        ],
        compiler_params=pltpu.CompilerParams(vmem_limit_bytes=28 << 20),
        name="block",
    )(r, win, pick, w, u, own_g, own_feat, own_d, b_in, gain, b_mid)


def solution(mesh):
    tm_count, n = mesh.shape["tm"], mesh.shape["space"]

    def per_device(tokens, w_in, b_in, gain, w_mid, b_mid):
        made = exchange(tokens[:, :, 0], w_in, w_mid, b_in, gain, tm_count, n)
        return block(*made, b_in, gain, b_mid, tm_count, n)

    return jax.shard_map(
        per_device,
        mesh=mesh,
        in_specs=(P("tm", None, "space", None), P(), P(), P(), P(), P()),
        out_specs=P("tm", "space", None, None),
        check_vma=False,
    )
```

```python
import functools

import jax
import jax.numpy as jnp
from jax import lax
from jax.experimental import pallas as pl
from jax.experimental.pallas import tpu as pltpu
from jax.sharding import PartitionSpec as P

MESH = pl.DeviceIdType.MESH
C = 384
LAT = 16
COLS = 64
F32 = jnp.float32
BF16 = jnp.bfloat16
SPACE = (2, 4, 8)


def far_first():
    def hops(step):
        return sum(min(d, size - d) for d, size in zip(step, SPACE))

    steps = [(i, j, k) for i in range(SPACE[0]) for j in range(SPACE[1]) for k in range(SPACE[2])]
    return sorted(steps, key=hops, reverse=True)


def lay_out_columns(r_ref, tb, pick_ref, spread, g, first):
    came = jnp.concatenate([r_ref[tb, t].reshape(2 * COLS, 128) for t in range(3)], axis=1)
    laid = jnp.dot(came, pick_ref[...], preferred_element_type=F32)
    spread[:, 0:8, :] = jnp.zeros((6, 8, 128), F32)
    spread[:, 136:144, :] = jnp.zeros((6, 8, 128), F32)
    for k in range(6):
        spread[k, 8:136, :] = laid[:, 128 * k : 128 * (k + 1)]
    col = (lax.broadcasted_iota(jnp.int32, (COLS, 128), 1) // 16) % 4
    for h in range(2):
        for fp in range(2):
            for q in range(3):
                before, here, after = (
                    spread[3 * fp + q, pl.ds(8 + h + 2 * step, COLS, stride=2), :] for step in (-1, 0, 1)
                )
                both = jnp.where(col == 0, before, jnp.where(col == 3, after, here))
                g[first + 2 * h + fp, :, 128 * q : 128 * (q + 1)] = both.astype(BF16)


def first_products(frames, count, win_ref):
    both = []
    for pair in range(2):
        lanes = slice(128 * pair, 128 * pair + 256)
        left = jnp.concatenate([frames(a, lanes) for a in range(3)], axis=1)
        for row in range(2):
            both.append(
                jnp.dot(left, win_ref[:, 2 * C * row : 2 * C * (row + 1)], preferred_element_type=F32)
            )
    return both


def activate(both, sub, bias, half_gain, keeps, feat, d):
    for parity in range(2):
        for block_row in range(COLS // 16):
            rows = slice(COLS * sub + 16 * block_row, COLS * sub + 16 * (block_row + 1))
            s = []
            for rho in range(4):
                f = (both[rho][rows, C * parity : C * (parity + 1)] + bias).astype(BF16)
                if rho in (1, 2) and feat is not None:
                    feat[rho - 1, parity, 16 * block_row : 16 * (block_row + 1)] = f
                v = f.astype(F32)
                scale = lax.rsqrt(jnp.sum(v * v, axis=-1, keepdims=True) * (1.0 / C) + 1e-6)
                if keeps[rho] is not None:
                    scale = scale * keeps[rho]
                half = v * scale * half_gain
                s.append((half + half * jnp.tanh(half)).astype(BF16))
            start = 128 * sub + COLS * parity + 16 * block_row
            at = slice(start, start + 16)
            d[0, at] = s[0] - s[2]
            d[1, at] = s[1] + s[2]
            d[2, at] = s[2] - s[1]
            d[3, at] = s[1] - s[3]


def edges(n):
    me = lax.axis_index("space")
    return jnp.where(me == 0, 0.0, 1.0), None, None, jnp.where(me == n - 1, 0.0, 1.0)


def exchange_kernel(
    tm_count, n, tok_hbm, w_in_hbm, w_hbm, bin_hbm, gain_hbm,
    r_ref, win_ref, pick_ref, w_ref, u_ref, v_ref, g_ref, feat_ref, d_ref,
    tok, x, w_in, bin_ref, gain_ref, spread,
    send_sem, recv_sem, send_next, recv_prev, own_sem, tok_sem, w_in_sem, bin_sem, gain_sem, w_sem,
):
    tm = lax.axis_index("tm")
    me = lax.axis_index("space")
    copies = (
        pltpu.make_async_copy(tok_hbm, tok, tok_sem),
        pltpu.make_async_copy(w_in_hbm, w_in, w_in_sem),
        pltpu.make_async_copy(bin_hbm, bin_ref, bin_sem),
        pltpu.make_async_copy(gain_hbm, gain_ref, gain_sem),
        pltpu.make_async_copy(w_hbm, w_ref, w_sem),
    )
    for copy in copies:
        copy.start()

    _, ny, nz = SPACE
    place = (me // (ny * nz), (me // nz) % ny, me % nz)
    strides = (ny * nz, nz, 1)
    along = [[((place[d] + s) % SPACE[d]) * strides[d] for s in range(SPACE[d])] for d in range(3)]
    peers = [along[0][i] + along[1][j] + along[2][k] for i, j, k in far_first()]

    barrier = pltpu.get_barrier_semaphore()

    def signal(group):
        for peer in group:
            if peer is not peers[-1]:
                pl.semaphore_signal(barrier, inc=1, device_id=(tm, peer), device_id_type=MESH)

        @pl.when(tm > 0)
        def _():
            for peer in group:
                pl.semaphore_signal(barrier, inc=1, device_id=(tm - 1, peer), device_id_type=MESH)

    signal(peers[:40])

    win_ref[...] = jnp.zeros(win_ref.shape, BF16)

    lane = lax.broadcasted_iota(jnp.int32, (C, C), 1)
    have = lax.broadcasted_iota(jnp.int32, (C, C), 0)
    y, col, c = lane // 64, (lane // 16) % 4, lane % 16
    shift = jnp.where(me == 0, -1, jnp.where(me == n - 1, 1, 0))
    want = (y // 2 + shift) * 128 + (y % 2) * 32 + ((col + 1) % 2) * 16 + c
    for fp in range(2):
        pick_ref[:, C * fp : C * (fp + 1)] = jnp.where(have == want + 64 * fp, 1.0, 0.0).astype(BF16)

    copies[0].wait()
    for h in range(2):
        x[:, h, :] = jnp.concatenate([tok[2 * h], tok[2 * h + 1]], axis=1)
    signal(peers[40:])

    @pl.when(tm == 0)
    def _():
        r_ref[0] = jnp.zeros(r_ref.shape[1:], r_ref.dtype)

    def rows_for(peer):
        return x.at[pl.ds(jnp.clip(peer - 1, 0, n - 3), 3)]

    pl.semaphore_wait(barrier, n - 1 + n * (1 - tm // (tm_count - 1)))
    own = pltpu.make_async_copy(rows_for(me), r_ref.at[1, :, me], own_sem)
    own.start()

    for peer in peers[:-1]:
        pltpu.make_async_remote_copy(
            src_ref=rows_for(peer), dst_ref=r_ref.at[1, :, me], send_sem=send_sem, recv_sem=recv_sem,
            device_id=(tm, peer), device_id_type=MESH,
        ).start()

    @pl.when(tm < tm_count - 1)
    def _():
        for peer in peers:
            pltpu.make_async_remote_copy(
                src_ref=rows_for(peer), dst_ref=r_ref.at[0, :, me], send_sem=send_next, recv_sem=recv_prev,
                device_id=(tm + 1, peer), device_id_type=MESH,
            ).start()

    copies[1].wait()
    for a in range(3):
        for b in range(3):
            block = w_in[a, b].reshape(3 * LAT, C)
            for row in range(2):
                for parity in range(2):
                    start = ((a * 4 + b + row) * 4 + parity) * LAT
                    lanes = slice((2 * row + parity) * C, (2 * row + parity + 1) * C)
                    win_ref[start : start + 3 * LAT, lanes] = block

    copies[4].wait()

    @pl.loop(0, 18)
    def _(i):
        e, base = i // 6, (i % 6) * 64
        for k in range(4):
            rows = pl.ds(pl.multiple_of(base + 16 * k, 16), 16)
            by_row = []
            for a in range(3):
                w0, w1, w2 = (w_ref[a, b, e, rows].astype(F32) for b in range(3))
                outer = w0 + w2
                by_row.append((w0, outer + w1, outer - w1, w2))
            for eta in (1, 2):
                u_ref[eta - 1, 0, e, rows] = by_row[0][eta].astype(BF16)
                u_ref[eta - 1, 1, e, rows] = by_row[2][eta].astype(BF16)
            for eta in range(4):
                outer, inner = by_row[0][eta] + by_row[2][eta], by_row[1][eta]
                v_ref[0, eta, e, rows] = (outer + inner).astype(BF16)
                v_ref[1, eta, e, rows] = (outer - inner).astype(BF16)

    def await_all(half, count, sem):
        whole = r_ref.at[half, :, pl.ds(0, count)]
        pltpu.make_async_copy(whole, whole, sem).wait()

    own.wait()
    await_all(1, n - 1, recv_sem)

    copies[2].wait()
    copies[3].wait()
    lay_out_columns(r_ref, 1, pick_ref, spread, g_ref, 0)
    both = first_products(
        lambda a, lanes: g_ref[a : a + 2, :, lanes].reshape(2 * COLS, 256), 2, win_ref
    )
    bias = bin_ref[...].reshape(1, C)
    half_gain = 0.5 * gain_ref[...].reshape(1, C)
    for sub in range(2):
        activate(both, sub, bias, half_gain, edges(n), feat_ref.at[sub], d_ref)

    await_all(1, n - 1, send_sem)

    @pl.when(tm < tm_count - 1)
    def _():
        await_all(0, n, send_next)

    @pl.when(tm > 0)
    def _():
        await_all(0, n, recv_prev)


def exchange(tok, w_in, w, b_in, gain, tm_count, n):
    hbm = pl.BlockSpec(memory_space=pltpu.HBM)
    vm = pl.BlockSpec(memory_space=pltpu.VMEM)
    return pl.pallas_call(
        functools.partial(exchange_kernel, tm_count, n),
        out_shape=(
            jax.ShapeDtypeStruct((2, 3, n, 2, 128), BF16),
            jax.ShapeDtypeStruct((3 * 4 * 4 * LAT, 4 * C), BF16),
            jax.ShapeDtypeStruct((C, 2 * C), BF16),
            jax.ShapeDtypeStruct(w.shape, BF16),
            jax.ShapeDtypeStruct((2, 2, 3, C, C), BF16),
            jax.ShapeDtypeStruct((2, 4, 3, C, C), BF16),
            jax.ShapeDtypeStruct((4, COLS, C), BF16),
            jax.ShapeDtypeStruct((2, 2, 2, COLS, C), BF16),
            jax.ShapeDtypeStruct((4, 2 * 128, C), BF16),
        ),
        in_specs=[hbm] * 5,
        out_specs=[vm] * 9,
        scratch_shapes=[
            pltpu.VMEM(tok.shape, BF16),
            pltpu.VMEM((n, 2, 128), BF16),
            pltpu.VMEM(w_in.shape, BF16),
            pltpu.VMEM((C,), F32),
            pltpu.VMEM((C,), F32),
            pltpu.VMEM((6, 2 * COLS + 16, 128), F32),
        ]
        + [pltpu.SemaphoreType.DMA] * 10,
        compiler_params=pltpu.CompilerParams(collective_id=0, has_side_effects=True, vmem_limit_bytes=8 << 20),
        name="exchange",
    )(*(pltpu.with_memory_space_constraint(v, pltpu.HBM) for v in (tok, w_in, w, b_in, gain)))


def block_kernel(
    tm_count, n, r_ref, win_ref, pick_ref, w_ref, u_ref, v_ref, own_g, own_feat, own_d, bin_ref, gain_ref, bmid_ref,
    out_ref, spread, g, d, dd, feat, part, down, up, tmp, made, out_sem,
):
    down[:, :, :, 0:8, :] = jnp.zeros(down.shape[:3] + (8, 128), F32)
    up[:, :, :, COLS : COLS + 8, :] = jnp.zeros(up.shape[:3] + (8, 128), F32)
    lay_out_columns(r_ref, 0, pick_ref, spread, g, 0)

    def frames(first, lanes):
        before = [g[first:4, :, lanes].reshape((4 - first) * COLS, 256)]
        if first:
            before.append(own_g[0:first, :, lanes].reshape(first * COLS, 256))
        return jnp.concatenate(before, axis=0)

    both = first_products(frames, 4, win_ref)
    bias = bin_ref[...].reshape(1, C)
    half_gain = 0.5 * gain_ref[...].reshape(1, C)
    not_first = jnp.where(lax.axis_index("tm") == 0, 0.0, 1.0)
    inside = edges(n)
    early = [not_first if keep is None else keep * not_first for keep in inside]
    for frame in range(4):
        activate(
            both, frame, bias, half_gain, early if frame < 2 else inside, feat.at[frame - 2] if frame >= 2 else None, d
        )

    bmid = bmid_ref[...].reshape(1, C)
    cells = [(k, e) for k in range(3) for e in range(3)]

    def weight(xi, eta, k, e):
        lanes = slice(128 * k, 128 * (k + 1))
        if xi in (1, 2):
            return v_ref[xi - 1, eta, e, :, lanes]
        if eta in (1, 2):
            return u_ref[eta - 1, xi // 3, e, :, lanes]
        return w_ref[2 * (xi // 3), 2 * (eta // 3), e, :, lanes]

    def plane(eta, frame):
        if frame < 4:
            return d[eta, 128 * frame : 128 * (frame + 1)]
        return own_d[eta, 128 * (frame - 4) : 128 * (frame - 3)]

    for eta in range(4):
        for pair in range(2):
            at = slice(128 * pair, 128 * (pair + 1))
            f = [plane(eta, 2 * pair + i) for i in range(4)]
            dd[0, eta, at] = f[0] - f[2]
            dd[1, eta, at] = f[1] + f[2]
            dd[2, eta, at] = f[2] - f[1]
            dd[3, eta, at] = f[1] - f[3]

    def combine(m):
        return 0.5 * (m[1] + m[2]) + m[0], 0.5 * (m[1] - m[2]) - m[3]

    def mix(tile):
        here = cells[2 * tile : 2 * tile + 2]
        by_frame = []
        for xi in range(4):
            m = []
            for eta in range(4):
                right = jnp.concatenate([weight(xi, eta, k, e) for k, e in here], axis=1)
                m.append(jnp.dot(dd[xi, eta], right, preferred_element_type=F32))
            by_frame.append(combine(m))
        for y in range(2):
            total = combine([s[y] for s in by_frame])
            for place, (k, e) in enumerate(here):
                for frame in range(4):
                    rows = 128 * (frame // 2)
                    mine = total[frame % 2][rows : rows + 128, 128 * place : 128 * (place + 1)]
                    even, odd = mine[:COLS], mine[COLS:]
                    if e == 2:
                        up[y, k, frame, 0:COLS, :] = even
                    else:
                        part[y, 3 * k + e, 128 * frame : 128 * frame + COLS] = even
                    if e == 0:
                        down[y, k, frame, 8 : 8 + COLS, :] = odd
                    else:
                        part[y, 3 * k + e, 128 * frame + COLS : 128 * (frame + 1)] = odd

    def out_copy(k):
        at = (slice(None), slice(None), slice(None), slice(128 * k, 128 * (k + 1)))
        return pltpu.make_async_copy(made.at[at], out_ref.at[at], out_sem.at[k])

    def finish(k):
        ln = slice(128 * k, 128 * (k + 1))
        for frame in range(4):
            even_rows = slice(128 * frame, 128 * frame + COLS)
            odd_rows = slice(128 * frame + COLS, 128 * (frame + 1))
            have = feat.at[frame] if frame < 2 else own_feat.at[frame - 2]
            for y in range(2):
                even = down[y, k, frame, pl.ds(7, COLS), :] + part[y, 3 * k + 1, even_rows] + part[y, 3 * k + 2, odd_rows]
                odd = part[y, 3 * k, even_rows] + part[y, 3 * k + 1, odd_rows] + up[y, k, frame, pl.ds(1, COLS), :]
                even = have[y, 0, :, ln].astype(F32) + even + bmid[:, ln]
                odd = have[y, 1, :, ln].astype(F32) + odd + bmid[:, ln]
                slot = tmp.at[k, frame, y]
                slot[pl.ds(0, COLS, stride=2), :] = even
                slot[pl.ds(1, COLS, stride=2), :] = odd
                made[frame, y, :, ln] = slot[...].astype(BF16)
        out_copy(k).start()

    mix(0)
    mix(1)
    finish(0)
    mix(2)
    finish(1)
    mix(3)
    mix(4)
    finish(2)
    for k in range(3):
        out_copy(k).wait()


def block(r, win, pick, w, u, v, own_g, own_feat, own_d, b_in, gain, b_mid, tm_count, n):
    vm = pl.BlockSpec(memory_space=pltpu.VMEM)
    return pl.pallas_call(
        functools.partial(block_kernel, tm_count, n),
        out_shape=jax.ShapeDtypeStruct((4, 2, 2 * COLS, C), BF16),
        in_specs=[vm] * 12,
        out_specs=pl.BlockSpec(memory_space=pl.ANY),
        scratch_shapes=[
            pltpu.VMEM((6, 2 * COLS + 16, 128), F32),
            pltpu.VMEM((4, COLS, C), BF16),
            pltpu.VMEM((4, 4 * 128, C), BF16),
            pltpu.VMEM((4, 4, 2 * 128, C), BF16),
            pltpu.VMEM((2, 2, 2, COLS, C), BF16),
            pltpu.VMEM((2, 9, 512, 128), F32),
            pltpu.VMEM((2, 3, 4, COLS + 8, 128), F32),
            pltpu.VMEM((2, 3, 4, COLS + 8, 128), F32),
            pltpu.VMEM((3, 4, 2, 128, 128), F32),
            pltpu.VMEM((4, 2, 2 * COLS, C), BF16),
            pltpu.SemaphoreType.DMA((3,)),
        ],
        compiler_params=pltpu.CompilerParams(vmem_limit_bytes=22 << 20),
        name="block",
    )(r, win, pick, w, u, v, own_g, own_feat, own_d, b_in, gain, b_mid)


def solution(mesh):
    tm_count, n = mesh.shape["tm"], mesh.shape["space"]

    def per_device(tokens, w_in, b_in, gain, w_mid, b_mid):
        made = exchange(tokens[:, :, 0], w_in, w_mid, b_in, gain, tm_count, n)
        return block(*made, b_in, gain, b_mid, tm_count, n)

    return jax.shard_map(
        per_device,
        mesh=mesh,
        in_specs=(P("tm", None, "space", None), P(), P(), P(), P(), P()),
        out_specs=P("tm", "space", None, None),
        check_vma=False,
    )
```

```python
import functools

import jax
import jax.numpy as jnp
from jax import lax
from jax.experimental import pallas as pl
from jax.experimental.pallas import tpu as pltpu
from jax.sharding import PartitionSpec as P

MESH = pl.DeviceIdType.MESH
C = 384
LAT = 16
COLS = 64
F32 = jnp.float32
BF16 = jnp.bfloat16
SPACE = (2, 4, 8)


def far_first():
    def hops(step):
        return sum(min(d, size - d) for d, size in zip(step, SPACE))

    steps = [(i, j, k) for i in range(SPACE[0]) for j in range(SPACE[1]) for k in range(SPACE[2])]
    return sorted(steps, key=hops, reverse=True)


def lay_out_columns(r_ref, tb, pick_ref, spread, g, first):
    came = jnp.concatenate([r_ref[tb, t].reshape(2 * COLS, 128) for t in range(3)], axis=1)
    laid = jnp.dot(came, pick_ref[...], preferred_element_type=F32)
    spread[:, 0:8, :] = jnp.zeros((6, 8, 128), F32)
    spread[:, 136:144, :] = jnp.zeros((6, 8, 128), F32)
    for k in range(6):
        spread[k, 8:136, :] = laid[:, 128 * k : 128 * (k + 1)]
    col = (lax.broadcasted_iota(jnp.int32, (COLS, 128), 1) // 16) % 4
    for h in range(2):
        for fp in range(2):
            for q in range(3):
                before, here, after = (
                    spread[3 * fp + q, pl.ds(8 + h + 2 * step, COLS, stride=2), :] for step in (-1, 0, 1)
                )
                both = jnp.where(col == 0, before, jnp.where(col == 3, after, here))
                g[first + 2 * h + fp, :, 128 * q : 128 * (q + 1)] = both.astype(BF16)


def first_products(frames, count, win_ref):
    both = []
    for pair in range(2):
        lanes = slice(128 * pair, 128 * pair + 256)
        left = jnp.concatenate([frames(a, lanes) for a in range(3)], axis=1)
        for row in range(2):
            both.append(
                jnp.dot(left, win_ref[:, 2 * C * row : 2 * C * (row + 1)], preferred_element_type=F32)
            )
    return both


def activate(both, sub, bias, half_gain, keeps, feat, d):
    for parity in range(2):
        for block_row in range(COLS // 16):
            rows = slice(COLS * sub + 16 * block_row, COLS * sub + 16 * (block_row + 1))
            s = []
            for rho in range(4):
                f = (both[rho][rows, C * parity : C * (parity + 1)] + bias).astype(BF16)
                if rho in (1, 2) and feat is not None:
                    feat[rho - 1, parity, 16 * block_row : 16 * (block_row + 1)] = f
                v = f.astype(F32)
                scale = lax.rsqrt(jnp.sum(v * v, axis=-1, keepdims=True) * (1.0 / C) + 1e-6)
                if keeps[rho] is not None:
                    scale = scale * keeps[rho]
                half = v * scale * half_gain
                s.append((half + half * jnp.tanh(half)).astype(BF16))
            start = 128 * sub + COLS * parity + 16 * block_row
            at = slice(start, start + 16)
            d[0, at] = s[0] - s[2]
            d[1, at] = s[1] + s[2]
            d[2, at] = s[2] - s[1]
            d[3, at] = s[1] - s[3]


def edges(n):
    me = lax.axis_index("space")
    return jnp.where(me == 0, 0.0, 1.0), None, None, jnp.where(me == n - 1, 0.0, 1.0)


def exchange_kernel(
    tm_count, n, tok_hbm, w_in_hbm, w_hbm, bin_hbm, gain_hbm,
    r_ref, win_ref, pick_ref, w_ref, u_ref, v_ref, g_ref, feat_ref, d_ref,
    tok, x, w_in, bin_ref, gain_ref, spread,
    send_sem, recv_sem, send_next, recv_prev, own_sem, tok_sem, w_in_sem, bin_sem, gain_sem, w_sem,
):
    tm = lax.axis_index("tm")
    me = lax.axis_index("space")
    copies = (
        pltpu.make_async_copy(tok_hbm, tok, tok_sem),
        pltpu.make_async_copy(w_in_hbm, w_in, w_in_sem),
        pltpu.make_async_copy(bin_hbm, bin_ref, bin_sem),
        pltpu.make_async_copy(gain_hbm, gain_ref, gain_sem),
        pltpu.make_async_copy(w_hbm, w_ref, w_sem),
    )
    for copy in copies:
        copy.start()

    _, ny, nz = SPACE
    place = (me // (ny * nz), (me // nz) % ny, me % nz)
    strides = (ny * nz, nz, 1)
    along = [[((place[d] + s) % SPACE[d]) * strides[d] for s in range(SPACE[d])] for d in range(3)]
    peers = [along[0][i] + along[1][j] + along[2][k] for i, j, k in far_first()]

    barrier = pltpu.get_barrier_semaphore()

    def signal(group):
        for peer in group:
            if peer is not peers[-1]:
                pl.semaphore_signal(barrier, inc=1, device_id=(tm, peer), device_id_type=MESH)

        @pl.when(tm > 0)
        def _():
            for peer in group:
                pl.semaphore_signal(barrier, inc=1, device_id=(tm - 1, peer), device_id_type=MESH)

    signal(peers[:40])

    win_ref[...] = jnp.zeros(win_ref.shape, BF16)

    lane = lax.broadcasted_iota(jnp.int32, (C, C), 1)
    have = lax.broadcasted_iota(jnp.int32, (C, C), 0)
    y, col, c = lane // 64, (lane // 16) % 4, lane % 16
    shift = jnp.where(me == 0, -1, jnp.where(me == n - 1, 1, 0))
    want = (y // 2 + shift) * 128 + (y % 2) * 32 + ((col + 1) % 2) * 16 + c
    for fp in range(2):
        pick_ref[:, C * fp : C * (fp + 1)] = jnp.where(have == want + 64 * fp, 1.0, 0.0).astype(BF16)

    copies[0].wait()
    for h in range(2):
        x[:, h, :] = jnp.concatenate([tok[2 * h], tok[2 * h + 1]], axis=1)
    signal(peers[40:])

    @pl.when(tm == 0)
    def _():
        r_ref[0] = jnp.zeros(r_ref.shape[1:], r_ref.dtype)

    def rows_for(peer):
        return x.at[pl.ds(jnp.clip(peer - 1, 0, n - 3), 3)]

    pl.semaphore_wait(barrier, n - 1 + n * (1 - tm // (tm_count - 1)))
    own = pltpu.make_async_copy(rows_for(me), r_ref.at[1, :, me], own_sem)
    own.start()

    for peer in peers[:-1]:
        pltpu.make_async_remote_copy(
            src_ref=rows_for(peer), dst_ref=r_ref.at[1, :, me], send_sem=send_sem, recv_sem=recv_sem,
            device_id=(tm, peer), device_id_type=MESH,
        ).start()

    @pl.when(tm < tm_count - 1)
    def _():
        for peer in peers:
            pltpu.make_async_remote_copy(
                src_ref=rows_for(peer), dst_ref=r_ref.at[0, :, me], send_sem=send_next, recv_sem=recv_prev,
                device_id=(tm + 1, peer), device_id_type=MESH,
            ).start()

    copies[1].wait()
    for a in range(3):
        for b in range(3):
            block = w_in[a, b].reshape(3 * LAT, C)
            for row in range(2):
                for parity in range(2):
                    start = ((a * 4 + b + row) * 4 + parity) * LAT
                    lanes = slice((2 * row + parity) * C, (2 * row + parity + 1) * C)
                    win_ref[start : start + 3 * LAT, lanes] = block

    copies[4].wait()

    @pl.loop(0, 18)
    def _(i):
        e, base = i // 6, (i % 6) * 64
        for k in range(4):
            rows = pl.ds(pl.multiple_of(base + 16 * k, 16), 16)
            by_row = []
            for a in range(3):
                w0, w1, w2 = (w_ref[a, b, e, rows].astype(F32) for b in range(3))
                outer = w0 + w2
                by_row.append((w0, outer + w1, outer - w1, w2))
            for eta in (1, 2):
                u_ref[eta - 1, 0, e, rows] = by_row[0][eta].astype(BF16)
                u_ref[eta - 1, 1, e, rows] = by_row[2][eta].astype(BF16)
            for eta in range(4):
                outer, inner = by_row[0][eta] + by_row[2][eta], by_row[1][eta]
                v_ref[0, eta, e, rows] = (outer + inner).astype(BF16)
                v_ref[1, eta, e, rows] = (outer - inner).astype(BF16)

    def await_all(half, count, sem):
        whole = r_ref.at[half, :, pl.ds(0, count)]
        pltpu.make_async_copy(whole, whole, sem).wait()

    own.wait()
    await_all(1, n - 1, recv_sem)

    copies[2].wait()
    copies[3].wait()
    lay_out_columns(r_ref, 1, pick_ref, spread, g_ref, 0)
    both = first_products(
        lambda a, lanes: g_ref[a : a + 2, :, lanes].reshape(2 * COLS, 256), 2, win_ref
    )
    bias = bin_ref[...].reshape(1, C)
    half_gain = 0.5 * gain_ref[...].reshape(1, C)
    for sub in range(2):
        activate(both, sub, bias, half_gain, edges(n), feat_ref.at[sub], d_ref)

    await_all(1, n - 1, send_sem)

    @pl.when(tm < tm_count - 1)
    def _():
        await_all(0, n, send_next)

    @pl.when(tm > 0)
    def _():
        await_all(0, n, recv_prev)


def exchange(tok, w_in, w, b_in, gain, tm_count, n):
    hbm = pl.BlockSpec(memory_space=pltpu.HBM)
    vm = pl.BlockSpec(memory_space=pltpu.VMEM)
    return pl.pallas_call(
        functools.partial(exchange_kernel, tm_count, n),
        out_shape=(
            jax.ShapeDtypeStruct((2, 3, n, 2, 128), BF16),
            jax.ShapeDtypeStruct((3 * 4 * 4 * LAT, 4 * C), BF16),
            jax.ShapeDtypeStruct((C, 2 * C), BF16),
            jax.ShapeDtypeStruct(w.shape, BF16),
            jax.ShapeDtypeStruct((2, 2, 3, C, C), BF16),
            jax.ShapeDtypeStruct((2, 4, 3, C, C), BF16),
            jax.ShapeDtypeStruct((4, COLS, C), BF16),
            jax.ShapeDtypeStruct((2, 2, 2, COLS, C), BF16),
            jax.ShapeDtypeStruct((4, 2 * 128, C), BF16),
        ),
        in_specs=[hbm] * 5,
        out_specs=[vm] * 9,
        scratch_shapes=[
            pltpu.VMEM(tok.shape, BF16),
            pltpu.VMEM((n, 2, 128), BF16),
            pltpu.VMEM(w_in.shape, BF16),
            pltpu.VMEM((C,), F32),
            pltpu.VMEM((C,), F32),
            pltpu.VMEM((6, 2 * COLS + 16, 128), F32),
        ]
        + [pltpu.SemaphoreType.DMA] * 10,
        compiler_params=pltpu.CompilerParams(collective_id=0, has_side_effects=True, vmem_limit_bytes=8 << 20),
        name="exchange",
    )(*(pltpu.with_memory_space_constraint(v, pltpu.HBM) for v in (tok, w_in, w, b_in, gain)))


def block_kernel(
    tm_count, n, r_ref, win_ref, pick_ref, w_ref, u_ref, v_ref, own_g, own_feat, own_d, bin_ref, gain_ref, bmid_ref,
    out_ref, spread, g, d, dd, feat, part, down, up, tmp, made, out_sem,
):
    down[:, :, :, 0:8, :] = jnp.zeros(down.shape[:3] + (8, 128), F32)
    up[:, :, :, COLS : COLS + 8, :] = jnp.zeros(up.shape[:3] + (8, 128), F32)
    lay_out_columns(r_ref, 0, pick_ref, spread, g, 0)

    def frames(first, lanes):
        before = [g[first:4, :, lanes].reshape((4 - first) * COLS, 256)]
        if first:
            before.append(own_g[0:first, :, lanes].reshape(first * COLS, 256))
        return jnp.concatenate(before, axis=0)

    both = first_products(frames, 4, win_ref)
    bias = bin_ref[...].reshape(1, C)
    half_gain = 0.5 * gain_ref[...].reshape(1, C)
    not_first = jnp.where(lax.axis_index("tm") == 0, 0.0, 1.0)
    inside = edges(n)
    early = [not_first if keep is None else keep * not_first for keep in inside]
    for frame in range(4):
        activate(
            both, frame, bias, half_gain, early if frame < 2 else inside, feat.at[frame - 2] if frame >= 2 else None, d
        )

    bmid = bmid_ref[...].reshape(1, C)
    cells = [(k, e) for k in range(3) for e in range(3)]

    def weight(xi, eta, k, e):
        lanes = slice(128 * k, 128 * (k + 1))
        if xi in (1, 2):
            return v_ref[xi - 1, eta, e, :, lanes]
        if eta in (1, 2):
            return u_ref[eta - 1, xi // 3, e, :, lanes]
        return w_ref[2 * (xi // 3), 2 * (eta // 3), e, :, lanes]

    def plane(eta, frame):
        if frame < 4:
            return d[eta, 128 * frame : 128 * (frame + 1)]
        return own_d[eta, 128 * (frame - 4) : 128 * (frame - 3)]

    for eta in range(4):
        for pair in range(2):
            at = slice(128 * pair, 128 * (pair + 1))
            f = [plane(eta, 2 * pair + i) for i in range(4)]
            dd[0, eta, at] = f[0] - f[2]
            dd[1, eta, at] = f[1] + f[2]
            dd[2, eta, at] = f[2] - f[1]
            dd[3, eta, at] = f[1] - f[3]

    def combine(m):
        return 0.5 * (m[1] + m[2]) + m[0], 0.5 * (m[1] - m[2]) - m[3]

    def mix(tile):
        here = cells[2 * tile : 2 * tile + 2]
        by_frame = []
        for xi in range(4):
            m = []
            for eta in range(4):
                right = jnp.concatenate([weight(xi, eta, k, e) for k, e in here], axis=1)
                m.append(jnp.dot(dd[xi, eta], right, preferred_element_type=F32))
            by_frame.append(combine(m))
        for y in range(2):
            total = combine([s[y] for s in by_frame])
            for place, (k, e) in enumerate(here):
                for frame in range(4):
                    rows = 128 * (frame // 2)
                    mine = total[frame % 2][rows : rows + 128, 128 * place : 128 * (place + 1)]
                    even, odd = mine[:COLS], mine[COLS:]
                    if e == 2:
                        up[y, k, frame, 0:COLS, :] = even
                    else:
                        part[y, 3 * k + e, 128 * frame : 128 * frame + COLS] = even
                    if e == 0:
                        down[y, k, frame, 8 : 8 + COLS, :] = odd
                    else:
                        part[y, 3 * k + e, 128 * frame + COLS : 128 * (frame + 1)] = odd

    def out_copy(k, frame):
        at = (frame, slice(None), slice(None), slice(128 * k, 128 * (k + 1)))
        return pltpu.make_async_copy(made.at[at], out_ref.at[at], out_sem.at[k, frame])

    def finish(k):
        ln = slice(128 * k, 128 * (k + 1))
        for frame in range(4):
            even_rows = slice(128 * frame, 128 * frame + COLS)
            odd_rows = slice(128 * frame + COLS, 128 * (frame + 1))
            have = feat.at[frame] if frame < 2 else own_feat.at[frame - 2]
            for y in range(2):
                even = down[y, k, frame, pl.ds(7, COLS), :] + part[y, 3 * k + 1, even_rows] + part[y, 3 * k + 2, odd_rows]
                odd = part[y, 3 * k, even_rows] + part[y, 3 * k + 1, odd_rows] + up[y, k, frame, pl.ds(1, COLS), :]
                even = have[y, 0, :, ln].astype(F32) + even + bmid[:, ln]
                odd = have[y, 1, :, ln].astype(F32) + odd + bmid[:, ln]
                slot = tmp.at[k, frame, y]
                slot[pl.ds(0, COLS, stride=2), :] = even
                slot[pl.ds(1, COLS, stride=2), :] = odd
                made[frame, y, :, ln] = slot[...].astype(BF16)
            out_copy(k, frame).start()

    mix(0)
    mix(1)
    finish(0)
    mix(2)
    finish(1)
    mix(3)
    mix(4)
    finish(2)
    for k in range(3):
        for frame in range(4):
            out_copy(k, frame).wait()


def block(r, win, pick, w, u, v, own_g, own_feat, own_d, b_in, gain, b_mid, tm_count, n):
    vm = pl.BlockSpec(memory_space=pltpu.VMEM)
    return pl.pallas_call(
        functools.partial(block_kernel, tm_count, n),
        out_shape=jax.ShapeDtypeStruct((4, 2, 2 * COLS, C), BF16),
        in_specs=[vm] * 12,
        out_specs=pl.BlockSpec(memory_space=pl.ANY),
        scratch_shapes=[
            pltpu.VMEM((6, 2 * COLS + 16, 128), F32),
            pltpu.VMEM((4, COLS, C), BF16),
            pltpu.VMEM((4, 4 * 128, C), BF16),
            pltpu.VMEM((4, 4, 2 * 128, C), BF16),
            pltpu.VMEM((2, 2, 2, COLS, C), BF16),
            pltpu.VMEM((2, 9, 512, 128), F32),
            pltpu.VMEM((2, 3, 4, COLS + 8, 128), F32),
            pltpu.VMEM((2, 3, 4, COLS + 8, 128), F32),
            pltpu.VMEM((3, 4, 2, 128, 128), F32),
            pltpu.VMEM((4, 2, 2 * COLS, C), BF16),
            pltpu.SemaphoreType.DMA((3, 4)),
        ],
        compiler_params=pltpu.CompilerParams(vmem_limit_bytes=22 << 20),
        name="block",
    )(r, win, pick, w, u, v, own_g, own_feat, own_d, b_in, gain, b_mid)


def solution(mesh):
    tm_count, n = mesh.shape["tm"], mesh.shape["space"]

    def per_device(tokens, w_in, b_in, gain, w_mid, b_mid):
        made = exchange(tokens[:, :, 0], w_in, w_mid, b_in, gain, tm_count, n)
        return block(*made, b_in, gain, b_mid, tm_count, n)

    return jax.shard_map(
        per_device,
        mesh=mesh,
        in_specs=(P("tm", None, "space", None), P(), P(), P(), P(), P()),
        out_specs=P("tm", "space", None, None),
        check_vma=False,
    )
```
